128 devices in a mesh: seq: 16 (over x_lo, y, core), heads: 8 (over z, x_hi).
Axes of the slice: x: 4 (x_hi: 2, x_lo: 2; x = x_hi * 2 + x_lo), y: 4, z: 4, core: 2. Of those that a mesh axis runs over, the one named last changes fastest.
Arguments:
- hidden_in: bfloat16 [4096, 8192], P('seq', 'heads'), may hold values from -6 to 6
- queries: bfloat16 [4096, 8192], P('seq', 'heads'), as said below
- image_kv: bfloat16 [16, 2, 6528, 1024], P('seq', None, None, 'heads'), as said below
- out_weight: bfloat16 [8192, 8192], P('seq', 'heads'), may hold values from -0.0625 to 0.0625
- gate: float32 [1], replicated, may hold values from 0.4 to 1.2
- tile_counts: int32 [16], replicated, may hold values from 1 to 4, as said below
- owners: int32 [256], replicated, may hold values from 0 to 15, as said below
- starts: int32 [256], replicated, may hold values from 0 to 3, as said below
- norm_gain: float32 [8192], P('heads'), may hold values from 0.1 to 1.9
- norm_grad: bfloat16 [4096, 8192], P('seq', 'heads'), may hold values from -6 to 6
- stream_grad: bfloat16 [4096, 8192], P('seq', 'heads'), may hold values from -6 to 6
Outputs:
- hidden_out: bfloat16 [4096, 8192], P('seq', 'heads')
- stream_in_grad: float32 [4096, 8192], P('seq', 'heads')
The draws below stay inside these ranges and needn't reach their ends.
Inputs may be any that keep to these rules, and one draw needn't show every extreme that they name: `tile_counts`: tiles of each image; some image has 4 tiles in every draw. `owners`: the image (named by the seq index that owns it) that a block of 16 text rows attends to; of the 16 blocks of one seq index at most 2 name the same image, and in every draw some image is named by exactly 2 blocks of every seq index. `starts`: the first tile a block sees, below the tile count of the block's image; in every draw some block starts at tile 0 and some at tile 4 - 1. `image_kv`: keys and values are real-valued. real-valued queries.
All inputs are finite; a program needn't handle non-finite values.
Results may differ from the reference program's by a relative error of at most 0.007.
Values may be sent and summed in bfloat16 or wider, within the bound.
No kernel may reach another device: no remote copies, remote signals or barrier semaphores. Data moves between devices by JAX's collectives and lax.ppermute only.
A program may use at most 128 MiB of HBM per device.

```python
import math
import jax
import jax.numpy as jnp
from jax import lax

D = 8192
HEADS = 64
KV_HEADS = 8
HEAD_DIM = 128
TILE_TOK = 1601
TILES_MAX = 4
TOK_DEV = 256
BLOCKS_DEV = 16
CAP = 2
BLK = 16
KEY_CAP = 6528
TOKENS = 4096
NBLK = 256
N_SEQ = 16


def layout(key):
    base = jax.random.fold_in(key, 7)
    keys = jax.random.split(base, 10)
    counts = jax.random.randint(keys[0], (N_SEQ,), 1, TILES_MAX + 1)
    hottest = jax.random.randint(keys[2], (), 0, N_SEQ)
    fullest = (hottest + 1 + jax.random.randint(keys[9], (), 0, N_SEQ - 1)) % N_SEQ
    counts = jnp.where(jnp.arange(N_SEQ) == fullest, TILES_MAX, counts)
    slots = jnp.arange(N_SEQ * CAP)
    ranking = jax.random.randint(keys[3], (N_SEQ, N_SEQ * CAP), 0, 1 << 20) * (N_SEQ * CAP) + slots[None, :]
    ranking = jnp.where((slots // CAP == fullest)[None, :], -1 - slots[None, :], ranking)
    ranking = jnp.where((slots // CAP == hottest)[None, :], -(1 << 22) - slots[None, :], ranking)
    ordered = jnp.argsort(ranking, axis=1)[:, :BLOCKS_DEV]
    chosen = ordered // CAP
    mixing = jax.vmap(lambda sub: jax.random.permutation(sub, BLOCKS_DEV))(jax.random.split(keys[4], N_SEQ))
    owners = jnp.take_along_axis(chosen, mixing, axis=1).reshape(-1)
    span = counts[owners]
    starts = jax.random.randint(keys[5], (N_SEQ * BLOCKS_DEV,), 0, 1 << 20) % span
    total_blocks = N_SEQ * BLOCKS_DEV
    marked = (owners == fullest).astype(jnp.int32)
    first_full = jnp.argmax(marked)
    last_full = total_blocks - 1 - jnp.argmax(marked[::-1])
    places = jnp.arange(total_blocks)
    starts = jnp.where(places == first_full, TILES_MAX - 1, starts)
    starts = jnp.where(places == last_full, 0, starts)
    return (counts, owners, starts)


def draw_tile_counts(key, part):
    return layout(key)[0].astype(jnp.int32)


def draw_owners(key, part):
    return layout(key)[1].astype(jnp.int32)


def draw_starts(key, part):
    return layout(key)[2].astype(jnp.int32)


def draw_image_kv(key, part):
    body_key = jax.random.fold_in(key, 11)
    shape = (N_SEQ, 2, KEY_CAP, KV_HEADS * HEAD_DIM)
    factor = jnp.array([2.0, 4.0], jnp.float32).reshape(1, 2, 1, 1)
    values = jax.random.truncated_normal(body_key, -4.0, 4.0, shape, jnp.float32) * factor
    return values.astype(jnp.bfloat16)


def draw_queries(key, part):
    body_key = jax.random.fold_in(key, 13)
    shape = (N_SEQ * TOK_DEV, D)
    values = jax.random.truncated_normal(body_key, -4.0, 4.0, shape, jnp.float32)
    return values.astype(jnp.bfloat16)


def block_levels(own_key, shape, cuts, smallest, top_value):
    def one(position, parts):
        draws = jax.random.uniform(jax.random.fold_in(jax.random.fold_in(own_key, 6), position), (parts,), jnp.float32, smallest / len(cuts), top_value / len(cuts))
        return jnp.repeat(jnp.exp(draws), shape[position] // parts).reshape((-1,) + (1,) * (len(shape) - position - 1))

    factor_of = one(*cuts[0])
    for cut in cuts[1:]:
        factor_of = factor_of * one(*cut)
    return factor_of


def noise(key, shape, spread, limit, cuts=(), dtype=jnp.bfloat16):
    gain = block_levels(key, shape, cuts, -0.22, 0.18) if cuts else 1.0
    drawn = jax.random.normal(key, shape, jnp.float32) * spread * gain
    return jnp.minimum(jnp.maximum(drawn, -limit), limit).astype(dtype)


def setup_inputs(seed: int = 0) -> dict:
    key_list = jax.random.split(jax.random.key(seed), 12)
    return {
        "hidden_in": noise(key_list[0], (TOKENS, D), 1.0, 6.0, ((0, 16), (1, 8))),
        "queries": draw_queries(jax.random.fold_in(key_list[11], 71), 0),
        "image_kv": draw_image_kv(jax.random.fold_in(key_list[11], 71), 0),
        "out_weight": noise(key_list[3], (D, D), D ** -0.5, 0.0625, ((0, 16), (1, 8))),
        "gate": jnp.clip(jax.random.uniform(key_list[4], (1,), jnp.float32, 0.4, 1.2), 0.4, 1.2),
        "tile_counts": draw_tile_counts(jax.random.fold_in(key_list[11], 71), 0),
        "owners": draw_owners(jax.random.fold_in(key_list[11], 71), 0),
        "starts": draw_starts(jax.random.fold_in(key_list[11], 71), 0),
        "norm_gain": jnp.clip(1.0 + 0.18 * jax.random.normal(key_list[8], (D,), jnp.float32), 0.1, 1.9),
        "norm_grad": noise(key_list[9], (TOKENS, D), 1.0, 6.0, ((0, 16), (1, 8))),
        "stream_grad": noise(key_list[10], (TOKENS, D), 1.0, 6.0, ((0, 16), (1, 8))),
    }


EPS = 1e-05

def attend_block(block, image_kv, tile_counts):
    rows, image, first = block
    pair = lax.dynamic_index_in_dim(image_kv, image, 0, keepdims=False).astype(jnp.float32)
    keys = pair[0].reshape(KEY_CAP, KV_HEADS, HEAD_DIM)
    values = pair[1].reshape(KEY_CAP, KV_HEADS, HEAD_DIM)
    grouped = rows.astype(jnp.float32).reshape(BLK, KV_HEADS, HEADS // KV_HEADS, HEAD_DIM)
    scale = 1.0 / math.sqrt(HEAD_DIM)
    scores = jnp.einsum('rkgd,nkd->kgrn', grouped, keys) * scale
    spot = jnp.arange(KEY_CAP).astype(jnp.int32)
    last = lax.dynamic_index_in_dim(tile_counts, image, 0, keepdims=False) * TILE_TOK
    seen = jnp.logical_and(spot >= first * TILE_TOK, spot < last)
    scores = jnp.where(seen, scores, -jnp.inf)
    highest = lax.optimization_barrier(jnp.max(scores, axis=-1, keepdims=True))
    probs = jnp.exp(scores - highest)
    total = lax.optimization_barrier(jnp.sum(probs, axis=-1, keepdims=True))
    weights = lax.optimization_barrier(probs.astype(jnp.bfloat16)).astype(jnp.float32)
    mixed = jnp.einsum('kgrn,nkd->kgrd', weights, values) / total
    return jnp.transpose(mixed, (2, 0, 1, 3)).reshape(BLK, HEADS * HEAD_DIM).astype(jnp.bfloat16)

def reference(hidden_in, queries, image_kv, out_weight, gate, tile_counts, owners, starts, norm_gain, norm_grad, stream_grad):
    q_blocks = queries.reshape(NBLK, BLK, D)
    context = lax.map(lambda block: attend_block(block, image_kv, tile_counts), (q_blocks, owners, starts))
    context = context.reshape(TOKENS, D)
    branch = jnp.dot(context, out_weight, preferred_element_type=jnp.float32)
    hidden_out = (hidden_in.astype(jnp.float32) + jnp.tanh(gate[0]) * branch).astype(jnp.bfloat16)
    hidden = hidden_out.astype(jnp.float32)
    scaled = norm_gain.astype(jnp.float32)[None, :] * norm_grad.astype(jnp.float32)
    inverse = lax.rsqrt(lax.optimization_barrier(jnp.mean(hidden * hidden, axis=1, keepdims=True)) + EPS)
    project = lax.optimization_barrier(jnp.mean(hidden * scaled, axis=1, keepdims=True))
    stream_in_grad = stream_grad.astype(jnp.float32) + inverse * scaled - inverse ** 3 * project * hidden
    return (hidden_out, stream_in_grad)
```

```python
import functools
import math

import jax
import jax.numpy as jnp
from jax import lax
from jax.experimental import pallas as pl
from jax.experimental.pallas import tpu as pltpu
from jax.sharding import Mesh, PartitionSpec as P

D = 8192
HEAD_DIM = 128
TILE_TOK = 1601
TILE_STEP = 1600
KEY_CAP = 6528
KEY_BLK = 1664
BLOCKS_DEV = 16
CAP = 2
BLK = 16
SEQ = 16
SLOTS = SEQ * CAP
HEADS_DEV = 8
GROUP = 8
SUB = 512
LOW = -2.3e38
HIGH = 2.3e38
EPS = 1e-05
EXP2_SCALE = math.log2(math.e) / math.sqrt(HEAD_DIM)

SEQ_AXES = ("xl", "y", "core")
HEAD_AXES = ("z", "xh")
UP = [(i, (i + 1) % 4) for i in range(4)]
DOWN = [(i, (i - 1) % 4) for i in range(4)]
SWAP = [(0, 1), (1, 0)]


def dispatch_kernel(owner_ref, q_ref, out_ref, used):
    for o in range(SEQ):
        used[o] = 0

    def place(b, carry):
        o = owner_ref[b]
        r = used[o]
        used[o] = r + 1
        row = pl.multiple_of(b * BLK, BLK)
        out_ref[o, r] = q_ref[pl.ds(row, BLK), :]
        return carry

    lax.fori_loop(0, BLOCKS_DEV, place, 0)


def dispatch(my_owner, queries):
    rows, width = queries.shape
    return pl.pallas_call(
        dispatch_kernel,
        out_shape=jax.ShapeDtypeStruct((SEQ, CAP, BLK, width), queries.dtype),
        grid_spec=pltpu.PrefetchScalarGridSpec(
            num_scalar_prefetch=1,
            grid=(1,),
            in_specs=[pl.BlockSpec((rows, width), lambda i, *_: (0, 0))],
            out_specs=pl.BlockSpec((SEQ, CAP, BLK, width), lambda i, *_: (0, 0, 0, 0)),
            scratch_shapes=[pltpu.SMEM((SEQ,), jnp.int32)],
        ),
        name="dispatch",
    )(my_owner, queries)


def collect_kernel(owner_ref, c_ref, out_ref, used):
    for core in range(2):
        for o in range(SEQ):
            used[o] = 0

        def place(b, carry):
            o = owner_ref[core * BLOCKS_DEV + b]
            r = used[o]
            used[o] = r + 1
            row = pl.multiple_of((core * BLOCKS_DEV + b) * BLK, BLK)
            out_ref[pl.ds(row, BLK), :] = c_ref[o, core * CAP + r]
            return carry

        lax.fori_loop(0, BLOCKS_DEV, place, 0)


def collect(chip_owner, returned):
    width = returned.shape[-1]
    rows = 2 * BLOCKS_DEV * BLK
    return pl.pallas_call(
        collect_kernel,
        out_shape=jax.ShapeDtypeStruct((rows, width), returned.dtype),
        grid_spec=pltpu.PrefetchScalarGridSpec(
            num_scalar_prefetch=1,
            grid=(1,),
            in_specs=[pl.BlockSpec(returned.shape, lambda i, *_: (0, 0, 0, 0))],
            out_specs=pl.BlockSpec((rows, width), lambda i, *_: (0, 0)),
            scratch_shapes=[pltpu.SMEM((SEQ,), jnp.int32)],
        ),
        name="collect",
    )(chip_owner, returned)


def attend_kernel(order, first, meta, q_ref, kv_ref, o_ref, q_s, v_s, m_s, acc):
    n_active = meta[0]
    tiles = meta[1]
    rows = GROUP * HEADS_DEV * BLK
    slot_rows = HEADS_DEV * BLK
    v_s[:, :HEAD_DIM] = kv_ref[0, 1]
    v_s[:, HEAD_DIM:] = jnp.ones((KEY_CAP, HEAD_DIM), jnp.bfloat16)
    col = lax.broadcasted_iota(jnp.int32, (SUB, HEAD_DIM), 1)

    def group(g, carry):
        for i in range(GROUP):
            slot = order[g * GROUP + i]
            for h in range(HEADS_DEV):
                at = i * slot_rows + h * BLK
                q_s[at : at + BLK, :] = q_ref[slot, :, h * HEAD_DIM : (h + 1) * HEAD_DIM]
        m_s[...] = jnp.full_like(m_s, LOW)
        acc[...] = jnp.zeros_like(acc)

        def tile(t, inner):
            base = pl.multiple_of(t * TILE_STEP, BLK)
            keys = kv_ref[0, 0, pl.ds(base, KEY_BLK), :]
            for u in range(rows // SUB):
                part = slice(u * SUB, (u + 1) * SUB)
                s = lax.dot_general(
                    q_s[part, :],
                    keys,
                    (((1,), (1,)), ((), ())),
                    preferred_element_type=jnp.float32,
                )
                tail = KEY_BLK - HEAD_DIM
                head_cols = jnp.where(col >= t, s[:, :HEAD_DIM], LOW)
                tail_cols = jnp.where(col + tail < t + TILE_TOK, s[:, tail:], LOW)
                s = jnp.concatenate([head_cols, s[:, HEAD_DIM:tail], tail_cols], axis=1)
                old = m_s[part, :1]
                new = jnp.maximum(old, jnp.max(s, axis=1, keepdims=True))
                kept, shift = [], []
                for i in range(SUB // slot_rows):
                    seen = first[g * GROUP + u * (SUB // slot_rows) + i] <= t
                    cut = slice(i * slot_rows, (i + 1) * slot_rows)
                    kept.append(jnp.where(seen, new[cut], old[cut]))
                    shift.append(jnp.where(seen, new[cut], HIGH))
                new = jnp.concatenate(kept, axis=0)
                shift = jnp.concatenate(shift, axis=0)
                probs = jnp.exp2((s - shift) * EXP2_SCALE).astype(jnp.bfloat16)
                fade = jnp.exp2((old - new) * EXP2_SCALE)
                m_s[part, :] = jnp.broadcast_to(new, (SUB, HEAD_DIM))
                acc[part, :] = acc[part, :] * fade + jnp.dot(
                    probs, v_s[pl.ds(base, KEY_BLK), :], preferred_element_type=jnp.float32
                )
            return inner

        lax.fori_loop(first[g * GROUP], tiles, tile, 0)
        for i in range(GROUP):
            slot = order[g * GROUP + i]
            chip = lax.shift_right_logical(slot, 2)
            place = jnp.bitwise_and(slot, 3)
            for h in range(HEADS_DEV):
                at = i * slot_rows + h * BLK
                cut = slice(at, at + BLK)
                half, inside = divmod(h, HEADS_DEV // 2)
                o_ref[chip, half, place, :, inside * HEAD_DIM : (inside + 1) * HEAD_DIM] = (
                    acc[cut, :HEAD_DIM] / acc[cut, HEAD_DIM:]
                ).astype(jnp.bfloat16)
        return carry

    lax.fori_loop(0, lax.div(n_active + GROUP - 1, GROUP), group, 0)


def attend(order, first, meta, received, image_kv):
    rows = GROUP * HEADS_DEV * BLK
    out = (SEQ // 2, 2, 2 * CAP, BLK, HEADS_DEV * HEAD_DIM // 2)
    return pl.pallas_call(
        attend_kernel,
        out_shape=jax.ShapeDtypeStruct(out, jnp.bfloat16),
        grid_spec=pltpu.PrefetchScalarGridSpec(
            num_scalar_prefetch=3,
            grid=(1,),
            in_specs=[
                pl.BlockSpec(received.shape, lambda i, *_: (0, 0, 0)),
                pl.BlockSpec(image_kv.shape, lambda i, *_: (0, 0, 0, 0)),
            ],
            out_specs=pl.BlockSpec(out, lambda i, *_: (0, 0, 0, 0, 0)),
            scratch_shapes=[
                pltpu.VMEM((rows, HEAD_DIM), jnp.bfloat16),
                pltpu.VMEM((KEY_CAP, 2 * HEAD_DIM), jnp.bfloat16),
                pltpu.VMEM((rows, HEAD_DIM), jnp.float32),
                pltpu.VMEM((rows, 2 * HEAD_DIM), jnp.float32),
            ],
        ),
        compiler_params=pltpu.CompilerParams(vmem_limit_bytes=56 << 20),
        name="attend",
    )(order, first, meta, received, image_kv)


def project_kernel(count, start, pick, *refs):
    blocks, rest = refs[:count], refs[count:]
    weights = rest[0]
    out_ref = rest[-1]
    total = None
    for i in range(count):
        term = jnp.dot(blocks[i][...], weights[pick[i]], preferred_element_type=jnp.float32)
        total = term if total is None else total + term
    out_ref[...] = total if start else rest[1][...] + total


def project(pick, blocks, weights, total=None):
    rows, depth = blocks[0].shape
    cols = weights.shape[2]
    count = len(blocks)
    step = cols // 2
    args = [*blocks, weights] + ([] if total is None else [total])
    specs = [pl.BlockSpec((rows, depth), lambda j, *_: (0, 0)) for _ in blocks]
    specs.append(pl.BlockSpec((weights.shape[0], depth, step), lambda j, *_: (0, 0, j)))
    if total is not None:
        specs.append(pl.BlockSpec((rows, step), lambda j, *_: (0, j)))
    return pl.pallas_call(
        functools.partial(project_kernel, count, total is None),
        out_shape=jax.ShapeDtypeStruct((rows, cols), jnp.float32),
        grid_spec=pltpu.PrefetchScalarGridSpec(
            num_scalar_prefetch=1,
            grid=(cols // step,),
            in_specs=specs,
            out_specs=pl.BlockSpec((rows, step), lambda j, *_: (0, j)),
        ),
        input_output_aliases={} if total is None else {count + 2: 0},
        name="project",
    )(pick, *args)


def routing(owners, starts, here):
    owner_table = owners.reshape(SEQ, BLOCKS_DEV)
    start_table = starts.reshape(SEQ, BLOCKS_DEV)
    ids = jnp.arange(BLOCKS_DEV)
    arriving = owner_table == here
    earlier = ids[None, :] < ids[:, None]
    rank = jnp.sum((arriving[:, None, :] & earlier[None, :, :]).astype(jnp.int32), axis=2)
    hit = arriving[:, None, :] & (rank[:, None, :] == jnp.arange(CAP)[None, :, None])
    slot_start = jnp.sum(jnp.where(hit, start_table[:, None, :], 0), axis=2).reshape(SLOTS)
    active = jnp.any(hit, axis=2).reshape(SLOTS)
    slots = jnp.arange(SLOTS)
    key = jnp.where(active, slot_start, 8) * SLOTS + slots
    position = jnp.sum((key[None, :] < key[:, None]).astype(jnp.int32), axis=1)
    at = position[None, :] == slots[:, None]
    order = jnp.sum(jnp.where(at, slots[None, :], 0), axis=1)
    first = jnp.sum(jnp.where(at, slot_start[None, :], 0), axis=1)
    return order, first, jnp.sum(active.astype(jnp.int32))


def shift(x, axis, pairs):
    return lax.ppermute(x, axis, pairs)


def local(
    hidden_in,
    queries,
    image_kv,
    out_weight,
    gate,
    tile_counts,
    owners,
    starts,
    norm_gain,
    norm_grad,
    stream_grad,
):
    here = lax.axis_index(SEQ_AXES)
    core = lax.axis_index("core")
    z = lax.axis_index("z")
    xh = lax.axis_index("xh")
    width = queries.shape[1]
    chip_owner = lax.dynamic_slice_in_dim(owners, (here - core) * BLOCKS_DEV, 2 * BLOCKS_DEV)
    my_owner = lax.dynamic_slice_in_dim(owners, here * BLOCKS_DEV, BLOCKS_DEV)

    weights = lax.all_gather(out_weight, ("xl", "y"), axis=0)

    outgoing = dispatch(my_owner, queries)
    received = lax.all_to_all(outgoing, SEQ_AXES, split_axis=0, concat_axis=0, tiled=True)
    order, first, n_active = routing(owners, starts, here)
    tiles = lax.dynamic_index_in_dim(tile_counts, here, 0, keepdims=False)
    meta = jnp.stack([n_active, tiles])
    context = attend(order, first, meta, received.reshape(SLOTS, BLK, width), image_kv)
    context = context.reshape(SEQ, 2 * CAP, BLK, width // 2)
    returned = lax.all_to_all(context, SEQ_AXES, split_axis=0, concat_axis=0, tiled=True)
    own = collect(chip_owner, returned)

    half = own.shape[0] // 2
    across = shift(own, "xh", SWAP)
    below = shift(own, "z", UP)
    above = shift(own, "z", DOWN)
    across_below = shift(across, "z", UP)
    across_above = shift(across, "z", DOWN)
    far = (shift(below[:half], "z", UP), shift(above[half:], "z", DOWN))
    across_far = tuple(shift(part, "xh", SWAP) for part in far)
    other = 1 - xh

    def block(step, which):
        return ((z + step) % 4) * 2 + which

    pick = jnp.stack([block(0, xh), block(0, other), block(3, xh), block(1, xh)])
    total = project(pick, [own, across, below, above], weights)
    pick = jnp.stack([block(3, other), block(1, other), block(2, xh), block(2, other)])
    total = project(
        pick,
        [
            across_below,
            across_above,
            jnp.concatenate(far, axis=0),
            jnp.concatenate(across_far, axis=0),
        ],
        weights,
        total,
    )
    total = total.reshape(2, half, total.shape[1])
    mine = lax.dynamic_index_in_dim(total, core, 0, keepdims=False)
    theirs = lax.dynamic_index_in_dim(total, 1 - core, 0, keepdims=False)
    branch = mine + shift(theirs, "core", SWAP)

    hidden_out = (hidden_in.astype(jnp.float32) + jnp.tanh(gate[0]) * branch).astype(jnp.bfloat16)
    hidden = hidden_out.astype(jnp.float32)
    scaled = norm_gain[None, :] * norm_grad.astype(jnp.float32)
    sums = jnp.stack([jnp.sum(hidden * hidden, axis=1), jnp.sum(hidden * scaled, axis=1)])
    members = [(a, b) for a in range(4) for b in range(2)]
    pieces = [sums]
    for dz in range(4):
        for dx in range(2):
            if dz or dx:
                pairs = [(a * 2 + b, ((a + dz) % 4) * 2 + (b + dx) % 2) for a, b in members]
                pieces.append(shift(sums, HEAD_AXES, pairs))
    squares, product = functools.reduce(jnp.add, pieces)
    inverse = lax.rsqrt(squares / D + EPS)[:, None]
    project_mean = (product / D)[:, None]
    stream_in_grad = (
        stream_grad.astype(jnp.float32) + inverse * scaled - inverse**3 * project_mean * hidden
    )
    return (hidden_out, stream_in_grad)


def solution(mesh):
    fine = Mesh(mesh.devices.reshape(2, 4, 2, 4, 2), SEQ_AXES + HEAD_AXES)
    both = P(SEQ_AXES, HEAD_AXES)
    placed = (
        both,
        both,
        P(SEQ_AXES, None, None, HEAD_AXES),
        both,
        P(),
        P(),
        P(),
        P(),
        P(HEAD_AXES),
        both,
        both,
    )
    return jax.shard_map(
        local,
        mesh=fine,
        in_specs=placed,
        out_specs=(both, both),
        check_vma=False,
    )
```

```python
import functools
import math

import jax
import jax.numpy as jnp
from jax import lax
from jax.experimental import pallas as pl
from jax.experimental.pallas import tpu as pltpu
from jax.sharding import Mesh, PartitionSpec as P


D = 8192
HEAD_DIM = 128
TILE_TOK = 1601
TILE_STEP = 1600
KEY_CAP = 6528
KEY_BLK = 1664
BLOCKS_DEV = 16
CAP = 2
BLK = 16
SEQ = 16
SLOTS = SEQ * CAP
HEADS_DEV = 8
GROUP = 8
SUB = 512
LOW = -2.3e38
HIGH = 2.3e38
EPS = 1e-05
EXP2_SCALE = math.log2(math.e) / math.sqrt(HEAD_DIM)

SEQ_AXES = ("xl", "y", "core")
HEAD_AXES = ("z", "xh")
UP = [(i, (i + 1) % 4) for i in range(4)]
DOWN = [(i, (i - 1) % 4) for i in range(4)]
SWAP = [(0, 1), (1, 0)]


def vmem():
    return pl.BlockSpec(memory_space=pltpu.VMEM)


def smem():
    return pl.BlockSpec(memory_space=pltpu.SMEM)


def near(*arrays):
    return [pltpu.with_memory_space_constraint(x, pltpu.VMEM) for x in arrays]


LIMIT = pltpu.CompilerParams(vmem_limit_bytes=24 << 20)
SMALL = pltpu.CompilerParams(vmem_limit_bytes=8 << 20)


def dispatch_kernel(owner_ref, q_ref, out_ref, used):
    first = lax.axis_index(SEQ_AXES) * BLOCKS_DEV
    for o in range(SEQ):
        used[o] = 0

    def place(b, carry):
        o = owner_ref[first + b]
        r = used[o]
        used[o] = r + 1
        row = pl.multiple_of(b * BLK, BLK)
        out_ref[o, r] = q_ref[pl.ds(row, BLK), :]
        return carry

    lax.fori_loop(0, BLOCKS_DEV, place, 0)


def dispatch(owners, queries):
    return pl.pallas_call(
        dispatch_kernel,
        out_shape=pltpu.VMEM((SEQ, CAP, BLK, queries.shape[1]), queries.dtype),
        in_specs=[smem(), vmem()],
        out_specs=vmem(),
        scratch_shapes=[pltpu.SMEM((SEQ,), jnp.int32)],
        compiler_params=SMALL,
        name="dispatch",
    )(owners, queries)


def collect_kernel(owner_ref, c_ref, out_ref, used):
    core = lax.axis_index("core")
    first = (lax.axis_index(SEQ_AXES) - core) * BLOCKS_DEV
    for part in range(2):
        which = jnp.bitwise_xor(core, part)
        for o in range(SEQ):
            used[o] = 0

        def place(b, carry):
            o = owner_ref[first + which * BLOCKS_DEV + b]
            r = used[o]
            used[o] = r + 1
            row = pl.multiple_of((part * BLOCKS_DEV + b) * BLK, BLK)
            out_ref[pl.ds(row, BLK), :] = c_ref[o, which * CAP + r]
            return carry

        lax.fori_loop(0, BLOCKS_DEV, place, 0)


def collect(owners, returned):
    rows = 2 * BLOCKS_DEV * BLK
    return pl.pallas_call(
        collect_kernel,
        out_shape=pltpu.VMEM((rows, returned.shape[-1]), returned.dtype),
        in_specs=[smem(), vmem()],
        out_specs=vmem(),
        scratch_shapes=[pltpu.SMEM((SEQ,), jnp.int32)],
        compiler_params=SMALL,
        name="collect",
    )(owners, *near(returned))


def attend_kernel(late, order, first, meta, q_ref, *refs):
    if late:
        kv_s, _, o_ref, q_s, m_s, acc = refs
    else:
        kv_ref, o_ref, kv_s, q_keep, q_s, m_s, acc = refs
        kv_s[:, :HEAD_DIM] = kv_ref[0, 0]
        kv_s[:, HEAD_DIM : 2 * HEAD_DIM] = kv_ref[0, 1]
        kv_s[:, 2 * HEAD_DIM :] = jnp.ones((KEY_CAP, HEAD_DIM), jnp.bfloat16)
        q_keep[...] = q_ref[...]
    groups = lax.shift_right_logical(meta[0] + GROUP - 1, 3)
    middle = lax.shift_right_logical(groups + 1, 1)
    tiles = meta[1]
    rows = GROUP * HEADS_DEV * BLK
    slot_rows = HEADS_DEV * BLK
    col = lax.broadcasted_iota(jnp.int32, (SUB, HEAD_DIM), 1)

    def group(g, carry):
        for i in range(GROUP):
            slot = order[g * GROUP + i]
            for h in range(HEADS_DEV):
                at = i * slot_rows + h * BLK
                q_s[at : at + BLK, :] = q_ref[slot, :, h * HEAD_DIM : (h + 1) * HEAD_DIM]
        m_s[...] = jnp.full_like(m_s, LOW)
        acc[...] = jnp.zeros_like(acc)

        def tile(t, inner):
            base = pl.multiple_of(t * TILE_STEP, BLK)
            keys = kv_s[pl.ds(base, KEY_BLK), :HEAD_DIM]
            for u in range(rows // SUB):
                part = slice(u * SUB, (u + 1) * SUB)
                s = lax.dot_general(
                    q_s[part, :],
                    keys,
                    (((1,), (1,)), ((), ())),
                    preferred_element_type=jnp.float32,
                )
                tail = KEY_BLK - HEAD_DIM
                head_cols = jnp.where(col >= t, s[:, :HEAD_DIM], LOW)
                tail_cols = jnp.where(col + tail < t + TILE_TOK, s[:, tail:], LOW)
                s = jnp.concatenate([head_cols, s[:, HEAD_DIM:tail], tail_cols], axis=1)
                old = m_s[part, :1]
                new = jnp.maximum(old, jnp.max(s, axis=1, keepdims=True))
                kept, shifts = [], []
                for i in range(SUB // slot_rows):
                    seen = first[g * GROUP + u * (SUB // slot_rows) + i] <= t
                    cut = slice(i * slot_rows, (i + 1) * slot_rows)
                    kept.append(jnp.where(seen, new[cut], old[cut]))
                    shifts.append(jnp.where(seen, new[cut], HIGH))
                new = jnp.concatenate(kept, axis=0)
                high = jnp.concatenate(shifts, axis=0)
                probs = jnp.exp2((s - high) * EXP2_SCALE).astype(jnp.bfloat16)
                fade = jnp.exp2((old - new) * EXP2_SCALE)
                m_s[part, :] = jnp.broadcast_to(new, (SUB, HEAD_DIM))
                acc[part, :] = acc[part, :] * fade + jnp.dot(
                    probs,
                    kv_s[pl.ds(base, KEY_BLK), HEAD_DIM:],
                    preferred_element_type=jnp.float32,
                )
            return inner

        lax.fori_loop(first[g * GROUP], tiles, tile, 0)
        for i in range(GROUP):
            slot = order[g * GROUP + i]
            chip = lax.shift_right_logical(slot, 2)
            place = jnp.bitwise_and(slot, 3)
            for h in range(HEADS_DEV):
                at = i * slot_rows + h * BLK
                cut = slice(at, at + BLK)
                half, inside = divmod(h, HEADS_DEV // 2)
                o_ref[chip, half, place, :, inside * HEAD_DIM : (inside + 1) * HEAD_DIM] = (
                    acc[cut, :HEAD_DIM] / acc[cut, HEAD_DIM:]
                ).astype(jnp.bfloat16)
        return carry

    if late:
        lax.fori_loop(middle, groups, group, 0)
    else:
        lax.fori_loop(0, middle, group, 0)


def attend(order, first, meta, received=None, image_kv=None, earlier=None):
    rows = GROUP * HEADS_DEV * BLK
    late = earlier is not None
    out = pltpu.VMEM((SEQ // 2, 2, 2 * CAP, BLK, HEADS_DEV * HEAD_DIM // 2), jnp.bfloat16)
    if late:
        context, keys, slots = near(*earlier)
        operands = (slots, keys, context)
    else:
        operands = (*near(received), image_kv)
        keys = pltpu.VMEM((KEY_CAP, 3 * HEAD_DIM), jnp.bfloat16)
        slots = pltpu.VMEM(received.shape, received.dtype)
    return pl.pallas_call(
        functools.partial(attend_kernel, late),
        out_shape=out if late else (out, keys, slots),
        input_output_aliases={5: 0} if late else {},
        in_specs=[smem()] * 3 + [vmem()] * len(operands),
        out_specs=vmem() if late else (vmem(),) * 3,
        scratch_shapes=[
            pltpu.VMEM((rows, HEAD_DIM), jnp.bfloat16),
            pltpu.VMEM((rows, HEAD_DIM), jnp.float32),
            pltpu.VMEM((rows, 2 * HEAD_DIM), jnp.float32),
        ],
        compiler_params=LIMIT,
        cost_estimate=pl.CostEstimate(flops=10**10, transcendentals=10**7, bytes_accessed=10**7),
        name="attend_late" if late else "attend_early",
    )(order, first, meta, *operands)


def assemble_kernel(*refs):
    pieces, out_ref = refs[:-1], refs[-1]
    xl = lax.axis_index("xl")
    y = lax.axis_index("y")
    n = 0
    for col in range(2):
        for dy in (0, 3, 1, 2):
            at = jnp.bitwise_xor(xl, col) * 4 + jnp.bitwise_and(y + dy, 3)
            row = 0
            while row < 512:
                size = pieces[n].shape[0]
                out_ref[at, row : row + size, :] = pieces[n][...]
                row += size
                n += 1


def assemble(pieces):
    return pl.pallas_call(
        assemble_kernel,
        out_shape=pltpu.VMEM((8,) + (512, pieces[0].shape[1]), pieces[0].dtype),
        in_specs=[vmem()] * len(pieces),
        out_specs=vmem(),
        compiler_params=SMALL,
        name="assemble",
    )(*near(*pieces))


def weight_spot(dz, flip):
    z = jnp.bitwise_and(lax.axis_index("z") + dz, 3)
    return z * 2 + jnp.bitwise_xor(lax.axis_index("xh"), flip)


def project_first_kernel(own, below, above, across, w, out_ref):
    total = None
    for block, dz, flip in ((own, 0, 0), (below, 3, 0), (above, 1, 0), (across, 0, 1)):
        term = jnp.dot(block[...], w[weight_spot(dz, flip)], preferred_element_type=jnp.float32)
        total = term if total is None else total + term
    out_ref[...] = total


def project_first(own, below, above, across, weights):
    return pl.pallas_call(
        project_first_kernel,
        out_shape=pltpu.VMEM((own.shape[0], weights.shape[2]), jnp.float32),
        in_specs=[vmem()] * 5,
        out_specs=vmem(),
        compiler_params=LIMIT,
        name="project_first",
    )(*near(own, below, above, across, weights))


def project_last_kernel(below, above, far_a, far_b, over_a, over_b, w, total, keep_ref, give_ref):
    half = keep_ref.shape[0]
    full = total[...]
    far = jnp.concatenate([far_a[...], far_b[...]], axis=0)
    over = jnp.concatenate([over_a[...], over_b[...]], axis=0)
    for block, dz, flip in ((below[...], 3, 1), (above[...], 1, 1), (far, 2, 0), (over, 2, 1)):
        full += jnp.dot(block, w[weight_spot(dz, flip)], preferred_element_type=jnp.float32)
    keep_ref[...] = full[:half]
    give_ref[...] = full[half:]


def project_last(blocks, weights, total):
    shape = pltpu.VMEM((total.shape[0] // 2, total.shape[1]), jnp.float32)
    return pl.pallas_call(
        project_last_kernel,
        out_shape=(shape, shape),
        in_specs=[vmem()] * 8,
        out_specs=(vmem(), vmem()),
        compiler_params=LIMIT,
        name="project_last",
    )(*near(*blocks, weights, total))


def routing(owners, starts, here):
    owner_table = owners.reshape(SEQ, BLOCKS_DEV)
    start_table = starts.reshape(SEQ, BLOCKS_DEV)
    ids = jnp.arange(BLOCKS_DEV)
    arriving = owner_table == here
    earlier = ids[None, :] < ids[:, None]
    rank = jnp.sum((arriving[:, None, :] & earlier[None, :, :]).astype(jnp.int32), axis=2)
    hit = arriving[:, None, :] & (rank[:, None, :] == jnp.arange(CAP)[None, :, None])
    slot_start = jnp.sum(jnp.where(hit, start_table[:, None, :], 0), axis=2).reshape(SLOTS)
    active = jnp.any(hit, axis=2).reshape(SLOTS)
    slots = jnp.arange(SLOTS)
    key = jnp.where(active, slot_start, 8) * SLOTS + slots
    position = jnp.sum((key[None, :] < key[:, None]).astype(jnp.int32), axis=1)
    at = position[None, :] == slots[:, None]
    order = jnp.sum(jnp.where(at, slots[None, :], 0), axis=1)
    first = jnp.sum(jnp.where(at, slot_start[None, :], 0), axis=1)
    return order, first, jnp.sum(active.astype(jnp.int32))


def local(
    hidden_in,
    queries,
    image_kv,
    out_weight,
    gate,
    tile_counts,
    owners,
    starts,
    norm_gain,
    norm_grad,
    stream_grad,
):
    here = lax.axis_index(SEQ_AXES)
    width = queries.shape[1]
    half = out_weight.shape[0] // 2

    w = out_weight
    outgoing = dispatch(owners, queries)
    received = lax.all_to_all(outgoing, SEQ_AXES, split_axis=0, concat_axis=0, tiled=True)

    w_lo = lax.ppermute(w, "y", UP)
    w_hi = lax.ppermute(w, "y", DOWN)
    w_x = lax.ppermute(w, "xl", SWAP)

    order, first, n_active = routing(owners, starts, here)
    tiles = lax.dynamic_index_in_dim(tile_counts, here, 0, keepdims=False)
    meta = jnp.stack([n_active, tiles])
    slots = received.reshape(SLOTS, BLK, width)
    early = attend(order, first, meta, slots, image_kv)

    far_a = lax.ppermute(w_lo[:half], "y", UP)
    far_b = lax.ppermute(w_hi[half:], "y", DOWN)
    x_lo_a = lax.ppermute(w_x[:half], "y", UP)
    x_hi_a = lax.ppermute(w_x[:half], "y", DOWN)
    x_lo_b = lax.ppermute(w_lo[half:], "xl", SWAP)
    x_hi_b = lax.ppermute(w_hi[half:], "xl", SWAP)

    context = attend(order, first, meta, earlier=early)

    x_far_a = lax.ppermute(x_lo_a, "y", UP)
    x_far_b = lax.ppermute(far_b, "xl", SWAP)

    context = context.reshape(SEQ, 2 * CAP, BLK, width // 2)
    returned = lax.all_to_all(context, SEQ_AXES, split_axis=0, concat_axis=0, tiled=True)
    weights = assemble(
        (w, w_lo, w_hi, far_a, far_b)
        + (w_x, x_lo_a, x_lo_b, x_hi_a, x_hi_b, x_far_a, x_far_b)
    )
    own = collect(owners, returned)
    below = lax.ppermute(own, "z", UP)
    above = lax.ppermute(own, "z", DOWN)
    across = lax.ppermute(own, "xh", SWAP)
    rows = own.shape[0] // 2
    far_a = lax.ppermute(below[:rows], "z", UP)
    far_b = lax.ppermute(above[rows:], "z", DOWN)
    across_below = lax.ppermute(across, "z", UP)
    across_above = lax.ppermute(across, "z", DOWN)
    over_a = lax.ppermute(far_a, "xh", SWAP)
    over_b = lax.ppermute(far_b, "xh", SWAP)
    total = project_first(own, below, above, across, weights)
    blocks = (across_below, across_above, far_a, far_b, over_a, over_b)
    keep, give = project_last(blocks, weights, total)
    branch = keep + lax.ppermute(give, "core", SWAP)

    hidden_out = (hidden_in.astype(jnp.float32) + jnp.tanh(gate[0]) * branch).astype(jnp.bfloat16)
    hidden = hidden_out.astype(jnp.float32)
    scaled = norm_gain[None, :] * norm_grad.astype(jnp.float32)
    sums = jnp.stack([jnp.sum(hidden * hidden, axis=1), jnp.sum(hidden * scaled, axis=1)])
    copies = jnp.broadcast_to(sums[None], (8,) + sums.shape)
    copies = lax.all_to_all(copies, HEAD_AXES, split_axis=0, concat_axis=0, tiled=True)
    squares, product = jnp.sum(copies, axis=0)
    inverse = lax.rsqrt(squares / D + EPS)[:, None]
    project_mean = (product / D)[:, None]
    stream_in_grad = (
        stream_grad.astype(jnp.float32) + inverse * scaled - inverse**3 * project_mean * hidden
    )
    return (hidden_out, stream_in_grad)


def solution(mesh):
    fine = Mesh(mesh.devices.reshape(2, 4, 2, 4, 2), SEQ_AXES + HEAD_AXES)
    both = P(SEQ_AXES, HEAD_AXES)
    placed = (
        both,
        both,
        P(SEQ_AXES, None, None, HEAD_AXES),
        both,
        P(),
        P(),
        P(),
        P(),
        P(HEAD_AXES),
        both,
        both,
    )
    return jax.shard_map(
        local,
        mesh=fine,
        in_specs=placed,
        out_specs=(both, both),
        check_vma=False,
    )
```

```python
import functools
import math

import jax
import jax.numpy as jnp
from jax import lax
from jax.experimental import pallas as pl
from jax.experimental.pallas import tpu as pltpu
from jax.sharding import Mesh, PartitionSpec as P


D = 8192
HEAD_DIM = 128
TILE_TOK = 1601
TILE_STEP = 1600
KEY_CAP = 6528
KEY_BLK = 1664
BLOCKS_DEV = 16
CAP = 2
BLK = 16
SEQ = 16
SLOTS = SEQ * CAP
HEADS_DEV = 8
GROUP = 8
SUB = 512
LOW = -2.3e38
HIGH = 2.3e38
EPS = 1e-05
EXP2_SCALE = math.log2(math.e) / math.sqrt(HEAD_DIM)

SEQ_AXES = ("xl", "y", "core")
HEAD_AXES = ("z", "xh")
UP = [(i, (i + 1) % 4) for i in range(4)]
DOWN = [(i, (i - 1) % 4) for i in range(4)]
SWAP = [(0, 1), (1, 0)]


def vmem():
    return pl.BlockSpec(memory_space=pltpu.VMEM)


def smem():
    return pl.BlockSpec(memory_space=pltpu.SMEM)


def near(*arrays):
    return [pltpu.with_memory_space_constraint(x, pltpu.VMEM) for x in arrays]


LIMIT = pltpu.CompilerParams(vmem_limit_bytes=24 << 20)
SMALL = pltpu.CompilerParams(vmem_limit_bytes=12 << 20)


def dispatch_kernel(owner_ref, q_ref, out_ref, used):
    first = lax.axis_index(SEQ_AXES) * BLOCKS_DEV
    for o in range(SEQ):
        used[o] = 0

    def place(b, carry):
        o = owner_ref[first + b]
        r = used[o]
        used[o] = r + 1
        row = pl.multiple_of(b * BLK, BLK)
        out_ref[o, r] = q_ref[pl.ds(row, BLK), :]
        return carry

    lax.fori_loop(0, BLOCKS_DEV, place, 0)


def dispatch(owners, queries):
    return pl.pallas_call(
        dispatch_kernel,
        out_shape=pltpu.VMEM((SEQ, CAP, BLK, queries.shape[1]), queries.dtype),
        in_specs=[smem(), vmem()],
        out_specs=vmem(),
        scratch_shapes=[pltpu.SMEM((SEQ,), jnp.int32)],
        compiler_params=SMALL,
        name="dispatch",
    )(owners, queries)


def collect_kernel(owner_ref, c_ref, out_ref, used):
    core = lax.axis_index("core")
    first = (lax.axis_index(SEQ_AXES) - core) * BLOCKS_DEV
    for part in range(2):
        which = jnp.bitwise_xor(core, part)
        for o in range(SEQ):
            used[o] = 0

        def place(b, carry):
            o = owner_ref[first + which * BLOCKS_DEV + b]
            r = used[o]
            used[o] = r + 1
            row = pl.multiple_of((part * BLOCKS_DEV + b) * BLK, BLK)
            out_ref[pl.ds(row, BLK), :] = c_ref[o, which * CAP + r]
            return carry

        lax.fori_loop(0, BLOCKS_DEV, place, 0)


def collect(owners, returned):
    rows = 2 * BLOCKS_DEV * BLK
    return pl.pallas_call(
        collect_kernel,
        out_shape=pltpu.VMEM((rows, returned.shape[-1]), returned.dtype),
        in_specs=[smem(), vmem()],
        out_specs=vmem(),
        scratch_shapes=[pltpu.SMEM((SEQ,), jnp.int32)],
        compiler_params=SMALL,
        name="collect",
    )(owners, *near(returned))


def widen_kernel(kv_ref, out_ref):
    out_ref[:, :HEAD_DIM] = kv_ref[0, 0]
    out_ref[:, HEAD_DIM : 2 * HEAD_DIM] = kv_ref[0, 1]
    out_ref[:, 2 * HEAD_DIM :] = jnp.ones((KEY_CAP, HEAD_DIM), jnp.bfloat16)


def widen(image_kv):
    return pl.pallas_call(
        widen_kernel,
        out_shape=pltpu.VMEM((KEY_CAP, 3 * HEAD_DIM), jnp.bfloat16),
        in_specs=[vmem()],
        out_specs=vmem(),
        compiler_params=SMALL,
        name="widen",
    )(image_kv)


def attend_kernel(late, order, first, meta, q_ref, kv_s, *refs):
    if late:
        _, o_ref, q_s, m_s, acc = refs
    else:
        o_ref, q_keep, q_s, m_s, acc = refs
        q_keep[...] = q_ref[...]
    groups = lax.shift_right_logical(meta[0] + GROUP - 1, 3)
    middle = lax.shift_right_logical(groups + 1, 1)
    tiles = meta[1]
    rows = GROUP * HEADS_DEV * BLK
    slot_rows = HEADS_DEV * BLK
    col = lax.broadcasted_iota(jnp.int32, (SUB, HEAD_DIM), 1)

    def group(g, carry):
        for i in range(GROUP):
            slot = order[g * GROUP + i]
            for h in range(HEADS_DEV):
                at = i * slot_rows + h * BLK
                q_s[at : at + BLK, :] = q_ref[slot, :, h * HEAD_DIM : (h + 1) * HEAD_DIM]
        m_s[...] = jnp.full_like(m_s, LOW)
        acc[...] = jnp.zeros_like(acc)

        def tile(t, inner):
            base = pl.multiple_of(t * TILE_STEP, BLK)
            keys = kv_s[pl.ds(base, KEY_BLK), :HEAD_DIM]
            blocks = rows // SUB

            def scores(u):
                return lax.dot_general(
                    q_s[u * SUB : (u + 1) * SUB, :],
                    keys,
                    (((1,), (1,)), ((), ())),
                    preferred_element_type=jnp.float32,
                )

            ahead = scores(0)
            for u in range(blocks):
                part = slice(u * SUB, (u + 1) * SUB)
                s = ahead
                if u + 1 < blocks:
                    ahead = scores(u + 1)
                tail = KEY_BLK - HEAD_DIM
                head_cols = jnp.where(col >= t, s[:, :HEAD_DIM], LOW)
                tail_cols = jnp.where(col + tail < t + TILE_TOK, s[:, tail:], LOW)
                s = jnp.concatenate([head_cols, s[:, HEAD_DIM:tail], tail_cols], axis=1)
                old = m_s[part, :1]
                new = jnp.maximum(old, jnp.max(s, axis=1, keepdims=True))
                kept, shifts = [], []
                for i in range(SUB // slot_rows):
                    seen = first[g * GROUP + u * (SUB // slot_rows) + i] <= t
                    cut = slice(i * slot_rows, (i + 1) * slot_rows)
                    kept.append(jnp.where(seen, new[cut], old[cut]))
                    shifts.append(jnp.where(seen, new[cut], HIGH))
                new = jnp.concatenate(kept, axis=0)
                high = jnp.concatenate(shifts, axis=0)
                probs = jnp.exp2((s - high) * EXP2_SCALE).astype(jnp.bfloat16)
                fade = jnp.exp2((old - new) * EXP2_SCALE)
                m_s[part, :] = jnp.broadcast_to(new, (SUB, HEAD_DIM))
                acc[part, :] = acc[part, :] * fade + jnp.dot(
                    probs,
                    kv_s[pl.ds(base, KEY_BLK), HEAD_DIM:],
                    preferred_element_type=jnp.float32,
                )
            return inner

        lax.fori_loop(first[g * GROUP], tiles, tile, 0)
        for i in range(GROUP):
            slot = order[g * GROUP + i]
            chip = lax.shift_right_logical(slot, 2)
            place = jnp.bitwise_and(slot, 3)
            for h in range(HEADS_DEV):
                at = i * slot_rows + h * BLK
                cut = slice(at, at + BLK)
                half, inside = divmod(h, HEADS_DEV // 2)
                o_ref[chip, half, place, :, inside * HEAD_DIM : (inside + 1) * HEAD_DIM] = (
                    acc[cut, :HEAD_DIM] / acc[cut, HEAD_DIM:]
                ).astype(jnp.bfloat16)
        return carry

    if late:
        lax.fori_loop(middle, groups, group, 0)
    else:
        lax.fori_loop(0, middle, group, 0)


def attend(order, first, meta, received, keys, context=None):
    rows = GROUP * HEADS_DEV * BLK
    late = context is not None
    out = pltpu.VMEM((SEQ // 2, 2, 2 * CAP, BLK, HEADS_DEV * HEAD_DIM // 2), jnp.bfloat16)
    slots = pltpu.VMEM(received.shape, received.dtype)
    operands = near(received, keys, *([context] if late else []))
    return pl.pallas_call(
        functools.partial(attend_kernel, late),
        out_shape=out if late else (out, slots),
        input_output_aliases={5: 0} if late else {},
        in_specs=[smem()] * 3 + [vmem()] * len(operands),
        out_specs=vmem() if late else (vmem(),) * 2,
        scratch_shapes=[
            pltpu.VMEM((rows, HEAD_DIM), jnp.bfloat16),
            pltpu.VMEM((rows, HEAD_DIM), jnp.float32),
            pltpu.VMEM((rows, 2 * HEAD_DIM), jnp.float32),
        ],
        compiler_params=LIMIT,
        cost_estimate=pl.CostEstimate(flops=10**10, transcendentals=10**7, bytes_accessed=10**7),
        name="attend_late" if late else "attend_early",
    )(order, first, meta, *operands)


def assemble_kernel(*refs):
    pieces, out_ref = refs[:-1], refs[-1]
    xl = lax.axis_index("xl")
    y = lax.axis_index("y")
    n = 0
    for col in range(2):
        for dy in (0, 3, 1, 2):
            at = jnp.bitwise_xor(xl, col) * 4 + jnp.bitwise_and(y + dy, 3)
            row = 0
            while row < 512:
                size = pieces[n].shape[0]
                out_ref[at, row : row + size, :] = pieces[n][...]
                row += size
                n += 1


def assemble(pieces):
    return pl.pallas_call(
        assemble_kernel,
        out_shape=pltpu.VMEM((8,) + (512, pieces[0].shape[1]), pieces[0].dtype),
        in_specs=[vmem()] * len(pieces),
        out_specs=vmem(),
        compiler_params=SMALL,
        name="assemble",
    )(*near(*pieces))


def weight_spot(dz, flip):
    z = jnp.bitwise_and(lax.axis_index("z") + dz, 3)
    return z * 2 + jnp.bitwise_xor(lax.axis_index("xh"), flip)


def project_first_kernel(own, below, above, across, w, out_ref):
    total = None
    for block, dz, flip in ((own, 0, 0), (below, 3, 0), (above, 1, 0), (across, 0, 1)):
        term = jnp.dot(block[...], w[weight_spot(dz, flip)], preferred_element_type=jnp.float32)
        total = term if total is None else total + term
    out_ref[...] = total


def project_first(own, below, above, across, weights):
    return pl.pallas_call(
        project_first_kernel,
        out_shape=pltpu.VMEM((own.shape[0], weights.shape[2]), jnp.float32),
        in_specs=[vmem()] * 5,
        out_specs=vmem(),
        compiler_params=LIMIT,
        name="project_first",
    )(*near(own, below, above, across, weights))


def project_last_kernel(below, above, far_a, far_b, over_a, over_b, w, total, keep_ref, give_ref):
    half = keep_ref.shape[0]
    full = total[...]
    far = jnp.concatenate([far_a[...], far_b[...]], axis=0)
    over = jnp.concatenate([over_a[...], over_b[...]], axis=0)
    for block, dz, flip in ((below[...], 3, 1), (above[...], 1, 1), (far, 2, 0), (over, 2, 1)):
        full += jnp.dot(block, w[weight_spot(dz, flip)], preferred_element_type=jnp.float32)
    keep_ref[...] = full[:half]
    give_ref[...] = full[half:].astype(jnp.bfloat16)


def project_last(blocks, weights, total):
    shape = pltpu.VMEM((total.shape[0] // 2, total.shape[1]), jnp.float32)
    return pl.pallas_call(
        project_last_kernel,
        out_shape=(shape, pltpu.VMEM(shape.shape, jnp.bfloat16)),
        in_specs=[vmem()] * 8,
        out_specs=(vmem(), vmem()),
        compiler_params=LIMIT,
        name="project_last",
    )(*near(*blocks, weights, total))


def routing(owners, starts, here):
    owner_table = owners.reshape(SEQ, BLOCKS_DEV)
    start_table = starts.reshape(SEQ, BLOCKS_DEV)
    ids = jnp.arange(BLOCKS_DEV)
    arriving = owner_table == here
    earlier = ids[None, :] < ids[:, None]
    rank = jnp.sum((arriving[:, None, :] & earlier[None, :, :]).astype(jnp.int32), axis=2)
    hit = arriving[:, None, :] & (rank[:, None, :] == jnp.arange(CAP)[None, :, None])
    slot_start = jnp.sum(jnp.where(hit, start_table[:, None, :], 0), axis=2).reshape(SLOTS)
    active = jnp.any(hit, axis=2).reshape(SLOTS)
    slots = jnp.arange(SLOTS)
    key = jnp.where(active, slot_start, 8) * SLOTS + slots
    position = jnp.sum((key[None, :] < key[:, None]).astype(jnp.int32), axis=1)
    at = position[None, :] == slots[:, None]
    order = jnp.sum(jnp.where(at, slots[None, :], 0), axis=1)
    first = jnp.sum(jnp.where(at, slot_start[None, :], 0), axis=1)
    return order, first, jnp.sum(active.astype(jnp.int32))


def local(
    hidden_in,
    queries,
    image_kv,
    out_weight,
    gate,
    tile_counts,
    owners,
    starts,
    norm_gain,
    norm_grad,
    stream_grad,
):
    here = lax.axis_index(SEQ_AXES)
    width = queries.shape[1]
    half = out_weight.shape[0] // 2

    w = out_weight
    outgoing = dispatch(owners, queries)
    received = lax.all_to_all(outgoing, SEQ_AXES, split_axis=0, concat_axis=0, tiled=True)

    w_lo = lax.ppermute(w, "y", UP)
    w_hi = lax.ppermute(w, "y", DOWN)
    w_x = lax.ppermute(w, "xl", SWAP)

    order, first, n_active = routing(owners, starts, here)
    tiles = lax.dynamic_index_in_dim(tile_counts, here, 0, keepdims=False)
    meta = jnp.stack([n_active, tiles])
    slots = received.reshape(SLOTS, BLK, width)
    keys = widen(image_kv)
    context, slots = attend(order, first, meta, slots, keys)

    w_far = lax.ppermute(w_lo, "y", UP)
    x_hi = lax.ppermute(w_x, "y", DOWN)
    x_lo = lax.ppermute(w_lo, "xl", SWAP)

    context = attend(order, first, meta, slots, keys, context)

    x_far_a = lax.ppermute(w_far[:half], "xl", SWAP)
    x_far_b = lax.ppermute(x_lo[half:], "y", UP)

    context = context.reshape(SEQ, 2 * CAP, BLK, width // 2)
    returned = lax.all_to_all(context, SEQ_AXES, split_axis=0, concat_axis=0, tiled=True)
    weights = assemble((w, w_lo, w_hi, w_far, w_x, x_lo, x_hi, x_far_a, x_far_b))
    own = collect(owners, returned)
    below = lax.ppermute(own, "z", UP)
    above = lax.ppermute(own, "z", DOWN)
    across = lax.ppermute(own, "xh", SWAP)
    rows = own.shape[0] // 2
    far_a = lax.ppermute(below[:rows], "z", UP)
    far_b = lax.ppermute(above[rows:], "z", DOWN)
    across_below = lax.ppermute(across, "z", UP)
    across_above = lax.ppermute(across, "z", DOWN)
    over_a = lax.ppermute(far_a, "xh", SWAP)
    over_b = lax.ppermute(far_b, "xh", SWAP)
    total = project_first(own, below, above, across, weights)
    blocks = (across_below, across_above, far_a, far_b, over_a, over_b)
    keep, give = project_last(blocks, weights, total)
    branch = keep + lax.ppermute(give, "core", SWAP).astype(jnp.float32)

    hidden_out = (hidden_in.astype(jnp.float32) + jnp.tanh(gate[0]) * branch).astype(jnp.bfloat16)
    hidden = hidden_out.astype(jnp.float32)
    scaled = norm_gain[None, :] * norm_grad.astype(jnp.float32)
    sums = jnp.stack([jnp.sum(hidden * hidden, axis=1), jnp.sum(hidden * scaled, axis=1)])
    copies = jnp.broadcast_to(sums[None], (8,) + sums.shape)
    copies = lax.all_to_all(copies, HEAD_AXES, split_axis=0, concat_axis=0, tiled=True)
    squares, product = jnp.sum(copies, axis=0)
    inverse = lax.rsqrt(squares / D + EPS)[:, None]
    project_mean = (product / D)[:, None]
    stream_in_grad = (
        stream_grad.astype(jnp.float32) + inverse * scaled - inverse**3 * project_mean * hidden
    )
    return (hidden_out, stream_in_grad)


def solution(mesh):
    fine = Mesh(mesh.devices.reshape(2, 4, 2, 4, 2), SEQ_AXES + HEAD_AXES)
    both = P(SEQ_AXES, HEAD_AXES)
    placed = (
        both,
        both,
        P(SEQ_AXES, None, None, HEAD_AXES),
        both,
        P(),
        P(),
        P(),
        P(),
        P(HEAD_AXES),
        both,
        both,
    )
    return jax.shard_map(
        local,
        mesh=fine,
        in_specs=placed,
        out_specs=(both, both),
        check_vma=False,
    )
```

```python
import math

import jax
import jax.numpy as jnp
from jax import lax
from jax.experimental import pallas as pl
from jax.experimental.pallas import tpu as pltpu
from jax.sharding import Mesh, PartitionSpec as P


D = 8192
HEAD_DIM = 128
TILE_TOK = 1601
TILE_STEP = 1600
KEY_CAP = 6528
KEY_BLK = 1664
BLOCKS_DEV = 16
CAP = 2
BLK = 16
SEQ = 16
SLOTS = SEQ * CAP
HEADS_DEV = 8
GROUP = 8
SUB = 512
LOW = -2.3e38
HIGH = 2.3e38
EPS = 1e-05
EXP2_SCALE = math.log2(math.e) / math.sqrt(HEAD_DIM)

SEQ_AXES = ("xl", "y", "core")
HEAD_AXES = ("z", "xh")
UP = [(i, (i + 1) % 4) for i in range(4)]
DOWN = [(i, (i - 1) % 4) for i in range(4)]
SWAP = [(0, 1), (1, 0)]
SLANT = [(a * 4 + b, (1 - a) * 4 + (b + 1) % 4) for a in range(2) for b in range(4)]


def vmem():
    return pl.BlockSpec(memory_space=pltpu.VMEM)


def smem():
    return pl.BlockSpec(memory_space=pltpu.SMEM)


def near(*arrays):
    return [pltpu.with_memory_space_constraint(x, pltpu.VMEM) for x in arrays]


LIMIT = pltpu.CompilerParams(vmem_limit_bytes=28 << 20)
SMALL = pltpu.CompilerParams(vmem_limit_bytes=12 << 20)


def dispatch_kernel(owner_ref, q_ref, out_ref, used, sems):
    first = lax.axis_index(SEQ_AXES) * BLOCKS_DEV
    for o in range(SEQ):
        used[o] = 0

    copies = []
    for b in range(BLOCKS_DEV):
        o = owner_ref[first + b]
        r = used[o]
        used[o] = r + 1
        block = q_ref.at[b * BLK : (b + 1) * BLK, :]
        copies.append(pltpu.make_async_copy(block, out_ref.at[o, r], sems.at[b]))
        copies[-1].start()
    for copy in copies:
        copy.wait()


def dispatch(owners, queries):
    return pl.pallas_call(
        dispatch_kernel,
        out_shape=pltpu.VMEM((SEQ, CAP, BLK, queries.shape[1]), queries.dtype),
        in_specs=[smem(), pl.BlockSpec(memory_space=pltpu.HBM)],
        out_specs=vmem(),
        scratch_shapes=[pltpu.SMEM((SEQ,), jnp.int32), pltpu.SemaphoreType.DMA((BLOCKS_DEV,))],
        compiler_params=SMALL,
        name="dispatch",
    )(owners, pltpu.with_memory_space_constraint(queries, pltpu.HBM))


def collect_kernel(owner_ref, c_ref, out_ref, used):
    core = lax.axis_index("core")
    first = (lax.axis_index(SEQ_AXES) - core) * BLOCKS_DEV
    for part in range(2):
        which = jnp.bitwise_xor(core, part)
        for o in range(SEQ):
            used[o] = 0

        def place(b, carry):
            o = owner_ref[first + which * BLOCKS_DEV + b]
            r = used[o]
            used[o] = r + 1
            row = pl.multiple_of((part * BLOCKS_DEV + b) * BLK, BLK)
            out_ref[pl.ds(row, BLK), :] = c_ref[o, which * CAP + r]
            return carry

        lax.fori_loop(0, BLOCKS_DEV, place, 0)


def collect(owners, returned):
    rows = 2 * BLOCKS_DEV * BLK
    return pl.pallas_call(
        collect_kernel,
        out_shape=pltpu.VMEM((rows, returned.shape[-1]), returned.dtype),
        in_specs=[smem(), vmem()],
        out_specs=vmem(),
        scratch_shapes=[pltpu.SMEM((SEQ,), jnp.int32)],
        compiler_params=SMALL,
        name="collect",
    )(owners, *near(returned))


def attend_kernel(order, first, meta, q_ref, kv_ref, o_ref, k_s, v_s, q_s, m_s, acc, sems):
    load_k = pltpu.make_async_copy(kv_ref.at[0, 0], k_s, sems.at[0])
    load_v = pltpu.make_async_copy(kv_ref.at[0, 1], v_s.at[:, :HEAD_DIM], sems.at[1])
    load_k.start()
    load_v.start()
    v_s[:, HEAD_DIM:] = jnp.ones((KEY_CAP, HEAD_DIM), jnp.bfloat16)
    load_k.wait()
    load_v.wait()
    groups = lax.div(meta[0] + GROUP - 1, GROUP)
    tiles = meta[1]
    rows = GROUP * HEADS_DEV * BLK
    slot_rows = HEADS_DEV * BLK
    col = lax.broadcasted_iota(jnp.int32, (SUB, HEAD_DIM), 1)

    def group(g, carry):
        for i in range(GROUP):
            slot = order[g * GROUP + i]
            for h in range(HEADS_DEV):
                at = i * slot_rows + h * BLK
                q_s[at : at + BLK, :] = q_ref[slot, :, h * HEAD_DIM : (h + 1) * HEAD_DIM]
        m_s[...] = jnp.full_like(m_s, LOW)
        acc[...] = jnp.zeros_like(acc)

        def tile(t, inner):
            base = pl.multiple_of(t * TILE_STEP, BLK)
            keys = k_s[pl.ds(base, KEY_BLK), :]
            blocks = rows // SUB

            def scores(u):
                return lax.dot_general(
                    q_s[u * SUB : (u + 1) * SUB, :],
                    keys,
                    (((1,), (1,)), ((), ())),
                    preferred_element_type=jnp.float32,
                )

            ahead = scores(0)
            for u in range(blocks):
                part = slice(u * SUB, (u + 1) * SUB)
                s = ahead
                if u + 1 < blocks:
                    ahead = scores(u + 1)
                tail = KEY_BLK - HEAD_DIM
                head_cols = jnp.where(col >= t, s[:, :HEAD_DIM], LOW)
                tail_cols = jnp.where(col + tail < t + TILE_TOK, s[:, tail:], LOW)
                s = jnp.concatenate([head_cols, s[:, HEAD_DIM:tail], tail_cols], axis=1)
                old = m_s[part, :1]
                new = jnp.maximum(old, jnp.max(s, axis=1, keepdims=True))
                kept, shifts = [], []
                for i in range(SUB // slot_rows):
                    seen = first[g * GROUP + u * (SUB // slot_rows) + i] <= t
                    cut = slice(i * slot_rows, (i + 1) * slot_rows)
                    kept.append(jnp.where(seen, new[cut], old[cut]))
                    shifts.append(jnp.where(seen, new[cut], HIGH))
                new = jnp.concatenate(kept, axis=0)
                high = jnp.concatenate(shifts, axis=0)
                probs = jnp.exp2((s - high) * EXP2_SCALE).astype(jnp.bfloat16)
                fade = jnp.exp2((old - new) * EXP2_SCALE)
                m_s[part, :] = jnp.broadcast_to(new, (SUB, HEAD_DIM))
                acc[part, :] = acc[part, :] * fade + jnp.dot(
                    probs,
                    v_s[pl.ds(base, KEY_BLK), :],
                    preferred_element_type=jnp.float32,
                )
            return inner

        lax.fori_loop(first[g * GROUP], tiles, tile, 0)
        for i in range(GROUP):
            slot = order[g * GROUP + i]
            chip = lax.shift_right_logical(slot, 2)
            place = jnp.bitwise_and(slot, 3)
            for h in range(HEADS_DEV):
                at = i * slot_rows + h * BLK
                cut = slice(at, at + BLK)
                half, inside = divmod(h, HEADS_DEV // 2)
                o_ref[chip, half, place, :, inside * HEAD_DIM : (inside + 1) * HEAD_DIM] = (
                    acc[cut, :HEAD_DIM] / acc[cut, HEAD_DIM:]
                ).astype(jnp.bfloat16)
        return carry

    lax.fori_loop(0, groups, group, 0)


def attend(order, first, meta, received, image_kv):
    rows = GROUP * HEADS_DEV * BLK
    return pl.pallas_call(
        attend_kernel,
        out_shape=pltpu.VMEM((SEQ // 2, 2, 2 * CAP, BLK, HEADS_DEV * HEAD_DIM // 2), jnp.bfloat16),
        in_specs=[smem()] * 3 + [vmem(), pl.BlockSpec(memory_space=pltpu.HBM)],
        out_specs=vmem(),
        scratch_shapes=[
            pltpu.VMEM((KEY_CAP, HEAD_DIM), jnp.bfloat16),
            pltpu.VMEM((KEY_CAP, 2 * HEAD_DIM), jnp.bfloat16),
            pltpu.VMEM((rows, HEAD_DIM), jnp.bfloat16),
            pltpu.VMEM((rows, HEAD_DIM), jnp.float32),
            pltpu.VMEM((rows, 2 * HEAD_DIM), jnp.float32),
            pltpu.SemaphoreType.DMA((2,)),
        ],
        compiler_params=LIMIT,
        cost_estimate=pl.CostEstimate(flops=10**10, transcendentals=10**7, bytes_accessed=10**7),
        name="attend",
    )(
        order,
        first,
        meta,
        *near(received),
        pltpu.with_memory_space_constraint(image_kv, pltpu.HBM),
    )


def assemble_kernel(*refs):
    pieces, out_ref = refs[:-1], refs[-1]
    xl = lax.axis_index("xl")
    y = lax.axis_index("y")
    n = 0
    for col in range(2):
        for dy in (0, 3, 1, 2):
            at = jnp.bitwise_xor(xl, col) * 4 + jnp.bitwise_and(y + dy, 3)
            row = 0
            while row < 512:
                size = pieces[n].shape[0]
                out_ref[at, row : row + size, :] = pieces[n][...]
                row += size
                n += 1


def assemble(pieces):
    return pl.pallas_call(
        assemble_kernel,
        out_shape=pltpu.VMEM((8,) + (512, pieces[0].shape[1]), pieces[0].dtype),
        in_specs=[vmem()] * len(pieces),
        out_specs=vmem(),
        compiler_params=SMALL,
        name="assemble",
    )(*near(*pieces))


def weight_spot(dz, flip):
    z = jnp.bitwise_and(lax.axis_index("z") + dz, 3)
    return z * 2 + jnp.bitwise_xor(lax.axis_index("xh"), flip)


def project_first_kernel(own, below, above, across, w, out_ref):
    total = None
    for block, dz, flip in ((own, 0, 0), (below, 3, 0), (above, 1, 0), (across, 0, 1)):
        term = jnp.dot(block[...], w[weight_spot(dz, flip)], preferred_element_type=jnp.float32)
        total = term if total is None else total + term
    out_ref[...] = total


def project_first(own, below, above, across, weights):
    return pl.pallas_call(
        project_first_kernel,
        out_shape=pltpu.VMEM((own.shape[0], weights.shape[2]), jnp.float32),
        in_specs=[vmem()] * 5,
        out_specs=vmem(),
        compiler_params=LIMIT,
        name="project_first",
    )(*near(own, below, above, across, weights))


def project_last_kernel(below, above, far_a, far_b, over_a, over_b, w, total, keep_ref, give_ref):
    half = keep_ref.shape[0]
    full = total[...]
    far = jnp.concatenate([far_a[...], far_b[...]], axis=0)
    over = jnp.concatenate([over_a[...], over_b[...]], axis=0)
    for block, dz, flip in ((below[...], 3, 1), (above[...], 1, 1), (far, 2, 0), (over, 2, 1)):
        full += jnp.dot(block, w[weight_spot(dz, flip)], preferred_element_type=jnp.float32)
    keep_ref[...] = full[:half]
    give_ref[...] = full[half:].astype(jnp.bfloat16)


def project_last(blocks, weights, total):
    shape = pltpu.VMEM((total.shape[0] // 2, total.shape[1]), jnp.float32)
    return pl.pallas_call(
        project_last_kernel,
        out_shape=(shape, pltpu.VMEM(shape.shape, jnp.bfloat16)),
        in_specs=[vmem()] * 8,
        out_specs=(vmem(), vmem()),
        compiler_params=LIMIT,
        name="project_last",
    )(*near(*blocks, weights, total))


def routing(owners, starts, here):
    owner_table = owners.reshape(SEQ, BLOCKS_DEV)
    start_table = starts.reshape(SEQ, BLOCKS_DEV)
    ids = jnp.arange(BLOCKS_DEV)
    arriving = owner_table == here
    earlier = ids[None, :] < ids[:, None]
    rank = jnp.sum((arriving[:, None, :] & earlier[None, :, :]).astype(jnp.int32), axis=2)
    hit = arriving[:, None, :] & (rank[:, None, :] == jnp.arange(CAP)[None, :, None])
    slot_start = jnp.sum(jnp.where(hit, start_table[:, None, :], 0), axis=2).reshape(SLOTS)
    active = jnp.any(hit, axis=2).reshape(SLOTS)
    slots = jnp.arange(SLOTS)
    key = jnp.where(active, slot_start, 8) * SLOTS + slots
    position = jnp.sum((key[None, :] < key[:, None]).astype(jnp.int32), axis=1)
    at = position[None, :] == slots[:, None]
    order = jnp.sum(jnp.where(at, slots[None, :], 0), axis=1)
    first = jnp.sum(jnp.where(at, slot_start[None, :], 0), axis=1)
    return order, first, jnp.sum(active.astype(jnp.int32))


def local(
    hidden_in,
    queries,
    image_kv,
    out_weight,
    gate,
    tile_counts,
    owners,
    starts,
    norm_gain,
    norm_grad,
    stream_grad,
):
    here = lax.axis_index(SEQ_AXES)
    width = queries.shape[1]
    half = out_weight.shape[0] // 2

    w = out_weight
    outgoing = dispatch(owners, queries)
    received = lax.all_to_all(outgoing, SEQ_AXES, split_axis=0, concat_axis=0, tiled=True)

    w_lo = lax.ppermute(w, "y", UP)
    w_hi = lax.ppermute(w, "y", DOWN)
    w_x = lax.ppermute(w, "xl", SWAP)
    x_lo = lax.ppermute(w, ("xl", "y"), SLANT)

    order, first, n_active = routing(owners, starts, here)
    tiles = lax.dynamic_index_in_dim(tile_counts, here, 0, keepdims=False)
    meta = jnp.stack([n_active, tiles])
    slots = received.reshape(SLOTS, BLK, width)
    context = attend(order, first, meta, slots, image_kv)
    w_far = lax.ppermute(w_lo, "y", UP)
    x_hi = lax.ppermute(w_x, "y", DOWN)


    x_lo_top, x_hi_end = x_lo[:half], x_hi[half:]
    x_far_a = lax.ppermute(x_lo_top, "y", UP)
    x_far_b = lax.ppermute(x_hi_end, "y", DOWN)

    context = context.reshape(SEQ, 2 * CAP, BLK, width // 2)
    returned = lax.all_to_all(context, SEQ_AXES, split_axis=0, concat_axis=0, tiled=True)
    weights = assemble((w, w_lo, w_hi, w_far, w_x, x_lo, x_hi, x_far_a, x_far_b))
    own = collect(owners, returned)
    below = lax.ppermute(own, "z", UP)
    above = lax.ppermute(own, "z", DOWN)
    across = lax.ppermute(own, "xh", SWAP)
    rows = own.shape[0] // 2
    far_a = lax.ppermute(below[:rows], "z", UP)
    far_b = lax.ppermute(above[rows:], "z", DOWN)
    across_below = lax.ppermute(across, "z", UP)
    across_above = lax.ppermute(across, "z", DOWN)
    over_a = lax.ppermute(far_a, "xh", SWAP)
    over_b = lax.ppermute(far_b, "xh", SWAP)
    total = project_first(own, below, above, across, weights)
    blocks = (across_below, across_above, far_a, far_b, over_a, over_b)
    keep, give = project_last(blocks, weights, total)
    branch = keep + lax.ppermute(give, "core", SWAP).astype(jnp.float32)

    hidden_out = (hidden_in.astype(jnp.float32) + jnp.tanh(gate[0]) * branch).astype(jnp.bfloat16)
    hidden = hidden_out.astype(jnp.float32)
    scaled = norm_gain[None, :] * norm_grad.astype(jnp.float32)
    sums = jnp.stack([jnp.sum(hidden * hidden, axis=1), jnp.sum(hidden * scaled, axis=1)])
    copies = jnp.broadcast_to(sums[None], (8,) + sums.shape)
    copies = lax.all_to_all(copies, HEAD_AXES, split_axis=0, concat_axis=0, tiled=True)
    squares, product = jnp.sum(copies, axis=0)
    inverse = lax.rsqrt(squares / D + EPS)[:, None]
    project_mean = (product / D)[:, None]
    stream_in_grad = (
        stream_grad.astype(jnp.float32) + inverse * scaled - inverse**3 * project_mean * hidden
    )
    return (hidden_out, stream_in_grad)


def solution(mesh):
    fine = Mesh(mesh.devices.reshape(2, 4, 2, 4, 2), SEQ_AXES + HEAD_AXES)
    both = P(SEQ_AXES, HEAD_AXES)
    placed = (
        both,
        both,
        P(SEQ_AXES, None, None, HEAD_AXES),
        both,
        P(),
        P(),
        P(),
        P(),
        P(HEAD_AXES),
        both,
        both,
    )
    return jax.shard_map(
        local,
        mesh=fine,
        in_specs=placed,
        out_specs=(both, both),
        check_vma=False,
    )
```

```python
import math

import jax
import jax.numpy as jnp
from jax import lax
from jax.experimental import pallas as pl
from jax.experimental.pallas import tpu as pltpu
from jax.sharding import Mesh, PartitionSpec as P


D = 8192
HEAD_DIM = 128
TILE_TOK = 1601
TILE_STEP = 1600
KEY_CAP = 6528
KEY_BLK = 1664
BLOCKS_DEV = 16
CAP = 2
BLK = 16
SEQ = 16
SLOTS = SEQ * CAP
HEADS_DEV = 8
GROUP = 8
SUB = 512
LOW = -2.3e38
HIGH = 2.3e38
EPS = 1e-05
EXP2_SCALE = math.log2(math.e) / math.sqrt(HEAD_DIM)

SEQ_AXES = ("xl", "y", "core")
HEAD_AXES = ("z", "xh")
UP = [(i, (i + 1) % 4) for i in range(4)]
DOWN = [(i, (i - 1) % 4) for i in range(4)]
SWAP = [(0, 1), (1, 0)]
SLANT = [(a * 4 + b, (1 - a) * 4 + (b + 1) % 4) for a in range(2) for b in range(4)]


def vmem():
    return pl.BlockSpec(memory_space=pltpu.VMEM)


def smem():
    return pl.BlockSpec(memory_space=pltpu.SMEM)


def near(*arrays):
    return [pltpu.with_memory_space_constraint(x, pltpu.VMEM) for x in arrays]


LIMIT = pltpu.CompilerParams(vmem_limit_bytes=28 << 20)
SMALL = pltpu.CompilerParams(vmem_limit_bytes=12 << 20)


def dispatch_kernel(owner_ref, q_ref, out_ref, used, sems):
    first = lax.axis_index(SEQ_AXES) * BLOCKS_DEV
    for o in range(SEQ):
        used[o] = 0

    copies = []
    for b in range(BLOCKS_DEV):
        o = owner_ref[first + b]
        r = used[o]
        used[o] = r + 1
        block = q_ref.at[b * BLK : (b + 1) * BLK, :]
        copies.append(pltpu.make_async_copy(block, out_ref.at[o, r], sems.at[b]))
        copies[-1].start()
    for copy in copies:
        copy.wait()


def dispatch(owners, queries):
    return pl.pallas_call(
        dispatch_kernel,
        out_shape=pltpu.VMEM((SEQ, CAP, BLK, queries.shape[1]), queries.dtype),
        in_specs=[smem(), pl.BlockSpec(memory_space=pltpu.HBM)],
        out_specs=vmem(),
        scratch_shapes=[pltpu.SMEM((SEQ,), jnp.int32), pltpu.SemaphoreType.DMA((BLOCKS_DEV,))],
        compiler_params=SMALL,
        name="dispatch",
    )(owners, pltpu.with_memory_space_constraint(queries, pltpu.HBM))


def collect_kernel(owner_ref, c_ref, out_ref, used):
    core = lax.axis_index("core")
    first = (lax.axis_index(SEQ_AXES) - core) * BLOCKS_DEV
    for part in range(2):
        which = jnp.bitwise_xor(core, part)
        for o in range(SEQ):
            used[o] = 0

        def place(b, carry):
            o = owner_ref[first + which * BLOCKS_DEV + b]
            r = used[o]
            used[o] = r + 1
            row = pl.multiple_of((part * BLOCKS_DEV + b) * BLK, BLK)
            out_ref[pl.ds(row, BLK), :] = c_ref[o, which * CAP + r]
            return carry

        lax.fori_loop(0, BLOCKS_DEV, place, 0)


def collect(owners, returned):
    rows = 2 * BLOCKS_DEV * BLK
    return pl.pallas_call(
        collect_kernel,
        out_shape=pltpu.VMEM((rows, returned.shape[-1]), returned.dtype),
        in_specs=[smem(), vmem()],
        out_specs=vmem(),
        scratch_shapes=[pltpu.SMEM((SEQ,), jnp.int32)],
        compiler_params=SMALL,
        name="collect",
    )(owners, *near(returned))


def attend_kernel(order, first, meta, q_ref, kv_ref, o_ref, k_s, v_s, q_s, m_s, acc, sems):
    load_k = pltpu.make_async_copy(kv_ref.at[0, 0], k_s, sems.at[0])
    load_v = pltpu.make_async_copy(kv_ref.at[0, 1], v_s.at[:, :HEAD_DIM], sems.at[1])
    load_k.start()
    load_v.start()
    v_s[:, HEAD_DIM:] = jnp.ones((KEY_CAP, HEAD_DIM), jnp.bfloat16)
    load_k.wait()
    load_v.wait()
    groups = lax.div(meta[0] + GROUP - 1, GROUP)
    tiles = meta[1]
    rows = GROUP * HEADS_DEV * BLK
    slot_rows = HEADS_DEV * BLK
    col = lax.broadcasted_iota(jnp.int32, (SUB, HEAD_DIM), 1)

    def group(g, carry):
        for i in range(GROUP):
            slot = order[g * GROUP + i]
            for h in range(HEADS_DEV):
                at = i * slot_rows + h * BLK
                q_s[at : at + BLK, :] = q_ref[slot, :, h * HEAD_DIM : (h + 1) * HEAD_DIM]
        m_s[...] = jnp.full_like(m_s, LOW)
        acc[...] = jnp.zeros_like(acc)

        def tile(t, inner):
            base = pl.multiple_of(t * TILE_STEP, BLK)
            keys = k_s[pl.ds(base, KEY_BLK), :]
            blocks = rows // SUB

            def scores(u):
                return lax.dot_general(
                    q_s[u * SUB : (u + 1) * SUB, :],
                    keys,
                    (((1,), (1,)), ((), ())),
                    preferred_element_type=jnp.float32,
                )

            ahead = scores(0)
            for u in range(blocks):
                part = slice(u * SUB, (u + 1) * SUB)
                s = ahead
                if u + 1 < blocks:
                    ahead = scores(u + 1)
                tail = KEY_BLK - HEAD_DIM
                head_cols = jnp.where(col >= t, s[:, :HEAD_DIM], LOW)
                tail_cols = jnp.where(col + tail < t + TILE_TOK, s[:, tail:], LOW)
                s = jnp.concatenate([head_cols, s[:, HEAD_DIM:tail], tail_cols], axis=1)
                old = m_s[part, :1]
                new = jnp.maximum(old, jnp.max(s, axis=1, keepdims=True))
                kept, shifts = [], []
                for i in range(SUB // slot_rows):
                    seen = first[g * GROUP + u * (SUB // slot_rows) + i] <= t
                    cut = slice(i * slot_rows, (i + 1) * slot_rows)
                    kept.append(jnp.where(seen, new[cut], old[cut]))
                    shifts.append(jnp.where(seen, new[cut], HIGH))
                new = jnp.concatenate(kept, axis=0)
                high = jnp.concatenate(shifts, axis=0)
                probs = jnp.exp2((s - high) * EXP2_SCALE).astype(jnp.bfloat16)
                fade = jnp.exp2((old - new) * EXP2_SCALE)
                m_s[part, :] = jnp.broadcast_to(new, (SUB, HEAD_DIM))
                acc[part, :] = acc[part, :] * fade + jnp.dot(
                    probs,
                    v_s[pl.ds(base, KEY_BLK), :],
                    preferred_element_type=jnp.float32,
                )
            return inner

        lax.fori_loop(first[g * GROUP], tiles, tile, 0)
        for i in range(GROUP):
            slot = order[g * GROUP + i]
            chip = lax.shift_right_logical(slot, 2)
            place = jnp.bitwise_and(slot, 3)
            for h in range(HEADS_DEV):
                at = i * slot_rows + h * BLK
                cut = slice(at, at + BLK)
                half, inside = divmod(h, HEADS_DEV // 2)
                o_ref[chip, half, place, :, inside * HEAD_DIM : (inside + 1) * HEAD_DIM] = (
                    acc[cut, :HEAD_DIM] / acc[cut, HEAD_DIM:]
                ).astype(jnp.bfloat16)
        return carry

    lax.fori_loop(0, groups, group, 0)


def attend(order, first, meta, received, image_kv):
    rows = GROUP * HEADS_DEV * BLK
    return pl.pallas_call(
        attend_kernel,
        out_shape=pltpu.VMEM((SEQ // 2, 2, 2 * CAP, BLK, HEADS_DEV * HEAD_DIM // 2), jnp.bfloat16),
        in_specs=[smem()] * 3 + [vmem(), pl.BlockSpec(memory_space=pltpu.HBM)],
        out_specs=vmem(),
        scratch_shapes=[
            pltpu.VMEM((KEY_CAP, HEAD_DIM), jnp.bfloat16),
            pltpu.VMEM((KEY_CAP, 2 * HEAD_DIM), jnp.bfloat16),
            pltpu.VMEM((rows, HEAD_DIM), jnp.bfloat16),
            pltpu.VMEM((rows, HEAD_DIM), jnp.float32),
            pltpu.VMEM((rows, 2 * HEAD_DIM), jnp.float32),
            pltpu.SemaphoreType.DMA((2,)),
        ],
        compiler_params=LIMIT,
        cost_estimate=pl.CostEstimate(flops=10**10, transcendentals=10**7, bytes_accessed=10**7),
        name="attend",
    )(
        order,
        first,
        meta,
        *near(received),
        pltpu.with_memory_space_constraint(image_kv, pltpu.HBM),
    )


def assemble_kernel(*refs):
    pieces, out_ref = refs[:-1], refs[-1]
    xl = lax.axis_index("xl")
    y = lax.axis_index("y")
    n = 0
    for col in range(2):
        for dy in (0, 3, 1, 2):
            at = jnp.bitwise_xor(xl, col) * 4 + jnp.bitwise_and(y + dy, 3)
            row = 0
            while row < 512:
                size = pieces[n].shape[0]
                out_ref[at, row : row + size, :] = pieces[n][...]
                row += size
                n += 1


def assemble(pieces):
    return pl.pallas_call(
        assemble_kernel,
        out_shape=pltpu.VMEM((8,) + (512, pieces[0].shape[1]), pieces[0].dtype),
        in_specs=[vmem()] * len(pieces),
        out_specs=vmem(),
        compiler_params=SMALL,
        name="assemble",
    )(*near(*pieces))


def weight_spot(dz, flip):
    z = jnp.bitwise_and(lax.axis_index("z") + dz, 3)
    return z * 2 + jnp.bitwise_xor(lax.axis_index("xh"), flip)


def project_first_kernel(own, below, above, across, w, out_ref):
    total = None
    for block, dz, flip in ((own, 0, 0), (below, 3, 0), (above, 1, 0), (across, 0, 1)):
        term = jnp.dot(block[...], w[weight_spot(dz, flip)], preferred_element_type=jnp.float32)
        total = term if total is None else total + term
    out_ref[...] = total


def project_first(own, below, above, across, weights):
    return pl.pallas_call(
        project_first_kernel,
        out_shape=pltpu.VMEM((own.shape[0], weights.shape[2]), jnp.float32),
        in_specs=[vmem()] * 5,
        out_specs=vmem(),
        compiler_params=LIMIT,
        name="project_first",
    )(*near(own, below, above, across, weights))


def project_last_kernel(below, above, far_a, far_b, over_a, over_b, w, total, keep_ref, give_ref):
    half = keep_ref.shape[0]
    full = total[...]
    far = jnp.concatenate([far_a[...], far_b[...]], axis=0)
    over = jnp.concatenate([over_a[...], over_b[...]], axis=0)
    for block, dz, flip in ((below[...], 3, 1), (above[...], 1, 1), (far, 2, 0), (over, 2, 1)):
        full += jnp.dot(block, w[weight_spot(dz, flip)], preferred_element_type=jnp.float32)
    keep_ref[...] = full[:half]
    give_ref[...] = full[half:].astype(jnp.bfloat16)


def project_last(blocks, weights, total):
    shape = pltpu.VMEM((total.shape[0] // 2, total.shape[1]), jnp.float32)
    return pl.pallas_call(
        project_last_kernel,
        out_shape=(shape, pltpu.VMEM(shape.shape, jnp.bfloat16)),
        in_specs=[vmem()] * 8,
        out_specs=(vmem(), vmem()),
        compiler_params=LIMIT,
        name="project_last",
    )(*near(*blocks, weights, total))


def routing(owners, starts, here):
    owner_table = owners.reshape(SEQ, BLOCKS_DEV)
    start_table = starts.reshape(SEQ, BLOCKS_DEV)
    ids = jnp.arange(BLOCKS_DEV)
    arriving = owner_table == here
    earlier = ids[None, :] < ids[:, None]
    rank = jnp.sum((arriving[:, None, :] & earlier[None, :, :]).astype(jnp.int32), axis=2)
    hit = arriving[:, None, :] & (rank[:, None, :] == jnp.arange(CAP)[None, :, None])
    slot_start = jnp.sum(jnp.where(hit, start_table[:, None, :], 0), axis=2).reshape(SLOTS)
    active = jnp.any(hit, axis=2).reshape(SLOTS)
    slots = jnp.arange(SLOTS)
    key = jnp.where(active, slot_start, 8) * SLOTS + slots
    position = jnp.sum((key[None, :] < key[:, None]).astype(jnp.int32), axis=1)
    at = position[None, :] == slots[:, None]
    order = jnp.sum(jnp.where(at, slots[None, :], 0), axis=1)
    first = jnp.sum(jnp.where(at, slot_start[None, :], 0), axis=1)
    return order, first, jnp.sum(active.astype(jnp.int32))


def local(
    hidden_in,
    queries,
    image_kv,
    out_weight,
    gate,
    tile_counts,
    owners,
    starts,
    norm_gain,
    norm_grad,
    stream_grad,
):
    here = lax.axis_index(SEQ_AXES)
    width = queries.shape[1]
    half = out_weight.shape[0] // 2

    w = out_weight
    outgoing = dispatch(owners, queries)
    received = lax.all_to_all(outgoing, SEQ_AXES, split_axis=0, concat_axis=0, tiled=True)

    w_lo = lax.ppermute(w, "y", UP)
    w_hi = lax.ppermute(w, "y", DOWN)
    w_x = lax.ppermute(w, "xl", SWAP)
    x_lo = lax.ppermute(w, ("xl", "y"), SLANT)

    order, first, n_active = routing(owners, starts, here)
    tiles = lax.dynamic_index_in_dim(tile_counts, here, 0, keepdims=False)
    meta = jnp.stack([n_active, tiles])
    slots = received.reshape(SLOTS, BLK, width)
    context = attend(order, first, meta, slots, image_kv)
    far_a = lax.ppermute(w_lo[:half], "y", UP)
    far_b = lax.ppermute(w_hi[half:], "y", DOWN)
    x_far = lax.ppermute(x_lo, "y", UP)
    x_hi = lax.ppermute(w_x, "y", DOWN)


    context = context.reshape(SEQ, 2 * CAP, BLK, width // 2)
    returned = lax.all_to_all(context, SEQ_AXES, split_axis=0, concat_axis=0, tiled=True)
    weights = assemble((w, w_lo, w_hi, far_a, far_b, w_x, x_lo, x_hi, x_far))
    own = collect(owners, returned)
    below = lax.ppermute(own, "z", UP)
    above = lax.ppermute(own, "z", DOWN)
    across = lax.ppermute(own, "xh", SWAP)
    rows = own.shape[0] // 2
    far_a = lax.ppermute(below[:rows], "z", UP)
    far_b = lax.ppermute(above[rows:], "z", DOWN)
    across_below = lax.ppermute(across, "z", UP)
    across_above = lax.ppermute(across, "z", DOWN)
    over_a = lax.ppermute(far_a, "xh", SWAP)
    over_b = lax.ppermute(far_b, "xh", SWAP)
    total = project_first(own, below, above, across, weights)
    blocks = (across_below, across_above, far_a, far_b, over_a, over_b)
    keep, give = project_last(blocks, weights, total)
    branch = keep + lax.ppermute(give, "core", SWAP).astype(jnp.float32)

    hidden_out = (hidden_in.astype(jnp.float32) + jnp.tanh(gate[0]) * branch).astype(jnp.bfloat16)
    hidden = hidden_out.astype(jnp.float32)
    scaled = norm_gain[None, :] * norm_grad.astype(jnp.float32)
    sums = jnp.stack([jnp.sum(hidden * hidden, axis=1), jnp.sum(hidden * scaled, axis=1)])
    copies = jnp.broadcast_to(sums[None], (8,) + sums.shape)
    copies = lax.all_to_all(copies, HEAD_AXES, split_axis=0, concat_axis=0, tiled=True)
    squares, product = jnp.sum(copies, axis=0)
    inverse = lax.rsqrt(squares / D + EPS)[:, None]
    project_mean = (product / D)[:, None]
    stream_in_grad = (
        stream_grad.astype(jnp.float32) + inverse * scaled - inverse**3 * project_mean * hidden
    )
    return (hidden_out, stream_in_grad)


def solution(mesh):
    fine = Mesh(mesh.devices.reshape(2, 4, 2, 4, 2), SEQ_AXES + HEAD_AXES)
    both = P(SEQ_AXES, HEAD_AXES)
    placed = (
        both,
        both,
        P(SEQ_AXES, None, None, HEAD_AXES),
        both,
        P(),
        P(),
        P(),
        P(),
        P(HEAD_AXES),
        both,
        both,
    )
    return jax.shard_map(
        local,
        mesh=fine,
        in_specs=placed,
        out_specs=(both, both),
        check_vma=False,
    )
```
